32 devices in a mesh: gx: 8 (over y, x, core), gy: 4 (over z).
Axes of the slice: x: 2, y: 2, z: 4, core: 2. Of those that a mesh axis runs over, the one named last changes fastest.
Arguments:
- panel: bfloat16 [8, 4, 2, 128, 1024], P('gx', 'gy'), may hold values from -0.5 to 0.5
- corner_panel: bfloat16 [8, 4, 2, 24, 128], P('gx', 'gy'), may hold values from -0.5 to 0.5
- interface_diag: float32 [8, 4, 2, 1024], P('gx', 'gy'), may hold values from 0.5 to 2
- coarse_diag: float32 [8, 128], P('gx'), may hold values from 0.5 to 2
- scaling: float32 [8, 4, 8, 128], P('gx', 'gy'), may hold values from 0.5 to 2
- dual_rhs: float32 [8, 4, 8, 128], P('gx', 'gy'), may hold values from -6 to 6
- block_map: int32 [8, 4, 2, 8], P('gx', 'gy'), may hold values from 0 to 39
- corner_map: int32 [8, 4, 2, 24], P('gx', 'gy'), may hold values from 0 to 127
- counts: int32 [8, 4], P('gx', 'gy'), may hold values from 1 to 2, as said below
Outputs:
- multipliers: float32 [8, 4, 8, 128], P('gx', 'gy')
- residual: float32 [8, 4, 8, 128], P('gx', 'gy')
The draws below stay inside these ranges and needn't reach their ends.
Inputs may be any that keep to these rules, and one draw needn't show every extreme that they name: `counts`: every device holds one or more live subdomains in its first slots; some device has all 2 slots live and some has one.
All inputs are finite; a program needn't handle non-finite values.
Results may differ from the reference program's by a relative error of at most 0.0003.
Values sent between devices are 32-bit elements; how exact they have to be, the bound alone decides.
A program may use at most 64 MiB of HBM per device.

```python
import math
import jax
import jax.numpy as jnp
from jax import lax

NI = 1024
BLK = 128
NBLK = 8
NP = 128
SD_DEV = 2
MB_DEV = 8
NCOR = 24
NCO = 128
ITERS = 3
SUB_X = 8
SUB_Y = 4


def draw_counts(key, part):
    values = jax.random.randint(key, (SUB_X, SUB_Y), 1, SD_DEV + 1)
    values = values.at[0, 0].set(SD_DEV)
    values = values.at[SUB_X - 1, SUB_Y - 1].set(1)
    return values.astype(jnp.int32)


def with_ends(values, own_key, least, top_value):
    dims = values.shape
    spot = [jax.random.randint(jax.random.fold_in(own_key, axis), (), 0, dims[axis]) for axis in range(len(dims))]
    values = values.at[tuple(spot)].set(least)
    longest = dims.index(max(dims))
    spot[longest] = (spot[longest] + 1) % dims[longest]
    return values.at[tuple(spot)].set(top_value)


def steps_of(rng, dims, cuts, least, largest):
    level, own = 1.0, jax.random.fold_in(rng, 6)
    for axis_at, shards_of in cuts:
        steps = jnp.exp(jax.random.uniform(jax.random.fold_in(own, axis_at), (shards_of,), jnp.float32, least / len(cuts), largest / len(cuts)))
        level = level * jnp.repeat(steps, dims[axis_at] // shards_of).reshape([-1 if axis == axis_at else 1 for axis in range(len(dims))])
    return level


def centred(own_key, shape, width, reach, cuts=(), held_as=jnp.bfloat16):
    level = steps_of(own_key, shape, cuts, -0.22, 0.18) if cuts else 1.0
    entries = jax.random.normal(own_key, shape, jnp.float32) * width * level
    return jnp.minimum(jnp.maximum(entries, -reach), reach).astype(held_as)


def setup_inputs(seed: int = 0) -> dict:
    seeds = jax.random.split(jax.random.key(seed), 10)
    return {
        "panel": centred(seeds[0], (SUB_X, SUB_Y, SD_DEV, NP, NI), NP ** -0.5, 0.5, ((0, 8), (1, 4))),
        "corner_panel": centred(seeds[1], (SUB_X, SUB_Y, SD_DEV, NCOR, NP), NP ** -0.5, 0.5, ((0, 8), (1, 4))),
        "interface_diag": jnp.clip(jnp.exp(math.log(2.0) - 1.3862944 * jax.random.uniform(seeds[2], (SUB_X, SUB_Y, SD_DEV, NI), jnp.float32) ** steps_of(seeds[2], (SUB_X, SUB_Y, SD_DEV, NI), ((0, 8), (1, 4)), -0.2, 0.2)), 0.5, 2.0),
        "coarse_diag": jnp.clip(jnp.exp(math.log(2.0) - 1.3862944 * jax.random.uniform(seeds[3], (SUB_X, NCO), jnp.float32) ** steps_of(seeds[3], (SUB_X, NCO), ((0, 8),), -0.2, 0.2)), 0.5, 2.0),
        "scaling": jnp.clip(jnp.exp(math.log(2.0) - 1.3862944 * jax.random.uniform(seeds[4], (SUB_X, SUB_Y, MB_DEV, BLK), jnp.float32) ** steps_of(seeds[4], (SUB_X, SUB_Y, MB_DEV, BLK), ((0, 8), (1, 4)), -0.2, 0.2)), 0.5, 2.0),
        "dual_rhs": centred(seeds[5], (SUB_X, SUB_Y, MB_DEV, BLK), 1.0, 6.0, ((0, 8), (1, 4)), jnp.float32),
        "block_map": with_ends(jax.random.randint(seeds[6], (SUB_X, SUB_Y, SD_DEV, NBLK), 0, 5 * MB_DEV), jax.random.fold_in(seeds[6], 1), 0, (5 * MB_DEV) - 1).astype(jnp.int32),
        "corner_map": with_ends(jax.random.randint(seeds[7], (SUB_X, SUB_Y, SD_DEV, NCOR), 0, NCO), jax.random.fold_in(seeds[7], 1), 0, NCO - 1).astype(jnp.int32),
        "counts": draw_counts(jax.random.fold_in(seeds[9], 71), 0),
    }


def reference(panel, corner_panel, interface_diag, coarse_diag, scaling, dual_rhs, block_map, corner_map, counts):
    highest = lax.Precision.HIGHEST
    owned = MB_DEV
    live = (lax.iota(jnp.int32, SD_DEV)[None, None, :] < counts[:, :, None]).astype(jnp.float32)

    def corner_row(pieces):
        factor_row, corner_row_panel = pieces
        factor_wide = factor_row.astype(jnp.float32)
        corner_wide = corner_row_panel.astype(jnp.float32)
        rows_coupled = jnp.einsum('yscn,ysni->ysci', corner_wide, factor_wide, precision=highest)
        blocks_coupled = jnp.einsum('yscn,ysdn->yscd', corner_wide, corner_wide, precision=highest)
        return (rows_coupled, blocks_coupled)
    coupling, corner_block = lax.map(corner_row, (panel, corner_panel))
    corner_block = corner_block * live[:, :, :, None, None]
    corner_hot = (corner_map[..., None] == lax.iota(jnp.int32, NCO)).astype(jnp.float32)
    spread = jnp.einsum('xysco,xyscd->xysod', corner_hot, corner_block, precision=highest)
    assembled = jnp.einsum('xysod,xysdp->xop', spread, corner_hot, precision=highest)
    coarse_eye = (lax.iota(jnp.int32, NCO)[:, None] == lax.iota(jnp.int32, NCO)[None, :]).astype(jnp.float32)
    system = assembled + coarse_diag[:, :, None] * coarse_eye[None]
    factor = jnp.linalg.cholesky(system)
    signs = jnp.where(block_map < owned, 1.0, -1.0) * live[..., None]
    picker = (block_map[..., None] == lax.iota(jnp.int32, 5 * owned)).astype(jnp.float32) * signs[..., None]

    def local_row(pieces):
        factor_row, vector_row, diag_row = pieces
        factor_wide = factor_row.astype(jnp.float32)
        inner_rows = jnp.einsum('ysni,ysi->ysn', factor_wide, vector_row, precision=highest)
        return diag_row * vector_row + jnp.einsum('ysni,ysn->ysi', factor_wide, inner_rows, precision=highest)

    def solve_one(lower, right):
        return jax.scipy.linalg.cho_solve((lower, True), right)

    def operate(field):
        padded = jnp.pad(field, ((1, 1), (1, 1), (0, 0), (0, 0)))
        candidates = jnp.concatenate([field, padded[2:, 1:-1], padded[:-2, 1:-1], padded[1:-1, 2:], padded[1:-1, :-2]], axis=2)
        gathered = jnp.einsum('xysbk,xykc->xysbc', picker, candidates, precision=highest)
        gathered = gathered.reshape(SUB_X, SUB_Y, SD_DEV, NI)
        result = lax.map(local_row, (panel, gathered, interface_diag))
        corner_values = jnp.einsum('xysci,xysi->xysc', coupling, gathered, precision=highest) * live[..., None]
        coarse_right = jnp.einsum('xysco,xysc->xo', corner_hot, corner_values, precision=highest)
        coarse_sol = jax.vmap(solve_one)(factor, coarse_right)
        back_values = jnp.einsum('xysco,xo->xysc', corner_hot, coarse_sol, precision=highest)
        result = result + jnp.einsum('xysci,xysc->xysi', coupling, back_values, precision=highest)
        contrib = jnp.einsum('xysbk,xysbc->xykc', picker, result.reshape(SUB_X, SUB_Y, SD_DEV, NBLK, BLK), precision=highest)
        pads = [jnp.pad(contrib[:, :, k * owned:(k + 1) * owned], ((1, 1), (1, 1), (0, 0), (0, 0))) for k in range(1, 5)]
        image = field + contrib[:, :, :owned]
        image = image + pads[0][:-2, 1:-1] + pads[1][2:, 1:-1] + pads[2][1:-1, :-2] + pads[3][1:-1, 2:]
        return image
    multipliers = jnp.zeros_like(dual_rhs)
    residual = dual_rhs
    direction = scaling * residual
    norm_now = jnp.sum(residual * direction)
    for sweep_index in range(ITERS):
        image = operate(direction)
        alpha = norm_now / jnp.sum(direction * image)
        multipliers = multipliers + alpha * direction
        residual = dual_rhs - operate(multipliers)
        precond = scaling * residual
        norm_next = jnp.sum(residual * precond)
        direction = precond + norm_next / norm_now * direction
        norm_now = norm_next
    return (multipliers, residual)
```

```python
import functools

import jax
import jax.numpy as jnp
from jax import lax
from jax.experimental import pallas as pl
from jax.experimental.pallas import tpu as pltpu
from jax.sharding import PartitionSpec as P

ITERS = 3
SCALE = 2.0**-8
MESH = pl.DeviceIdType.MESH
HIGHEST = lax.Precision.HIGHEST


def invert_tile(mat, tile):
    size = mat.shape[0]
    base = tile * 128
    if not isinstance(base, int):
        base = pl.multiple_of(base, 128)
    lanes = lax.broadcasted_iota(jnp.int32, (8, size), 1) - base
    subs = lax.broadcasted_iota(jnp.int32, (8, size), 0)
    narrow = lax.broadcasted_iota(jnp.int32, (8, 128), 0)
    for block in range(16):
        first = 8 * block
        rows = mat[pl.ds(base + first, 8), :]
        small = mat[pl.ds(base + first, 8), pl.ds(base, 128)]
        cols = [
            jnp.broadcast_to(small[:, first + c : first + c + 1], (8, 128)) for c in range(8)
        ]
        inside = (lanes >= first) & (lanes < first + 8)
        rows = jnp.where(inside, (lanes - first == subs).astype(jnp.float32), rows)
        for k in range(8):
            inverse = 1.0 / cols[k][k : k + 1, :]
            factor = cols[k]
            scaled = rows[k : k + 1, :] * jnp.tile(inverse, (1, size // 128))
            wide = jnp.tile(factor, (1, size // 128))
            rows = jnp.where(subs == k, scaled, rows - wide * scaled)
            for c in range(k + 1, 8):
                own = cols[c][k : k + 1, :] * inverse
                cols[c] = jnp.where(narrow == k, own, cols[c] - factor * own)

        def update(start, count):
            panel = mat[pl.ds(start, count), pl.ds(base, 128)]
            old = mat[pl.ds(start, count), :]
            total = jnp.where(inside[0:1, :], 0.0, old)
            for c in range(8):
                total = total - panel[:, first + c : first + c + 1] * rows[c : c + 1, :]
            mat[pl.ds(start, count), :] = total

        if size == 128:
            update(0, size)
        else:
            @pl.loop(0, size // 8)
            def _(chunk):
                update(pl.multiple_of(chunk * 8, 8), 8)

        mat[pl.ds(base + first, 8), :] = rows


def combine(moments):
    inverse_scale = 1.0 / SCALE
    res = [jnp.ones_like(moments[0])]
    direc = [jnp.ones_like(moments[0])]
    mult = []
    norm = moments[0]

    def form(left, right, shift):
        total = None
        for i, a in enumerate(left):
            for j, b in enumerate(right):
                term = a * b * moments[i + j + shift]
                total = term if total is None else total + term
        return total

    for step in range(ITERS):
        energy = form(direc, direc, 1) * inverse_scale
        alpha = norm / energy
        mult = [
            (mult[i] if i < len(mult) else 0.0) + alpha * direc[i] for i in range(len(direc))
        ]
        image = [None] + [d * inverse_scale for d in direc]
        res = [
            (res[i] if i < len(res) else 0.0)
            - (alpha * image[i] if image[i] is not None else 0.0)
            for i in range(len(image))
        ]
        if step < ITERS - 1:
            after = form(res, res, 0)
            beta = after / norm
            direc = [res[i] + (beta * direc[i] if i < len(direc) else 0.0) for i in range(len(res))]
            norm = after
    return mult, res


def kernel(
    nx,
    ny,
    block_map,
    counts,
    panel,
    corner,
    diag,
    coarse_diag,
    scaling,
    rhs,
    map_rows,
    corner_map,
    mult_out,
    res_out,
    cand,
    contrib,
    inbox,
    wide,
    pick,
    part,
    mat,
    expand,
    spread,
    gpart,
    red_x,
    red_y,
    halo_send,
    halo_recv,
    back_send,
    back_recv,
    mat_send,
    mat_recv,
    g_send,
    g_recv,
    rx_send,
    rx_recv,
    ry_send,
    ry_recv,
):
    slots, rows, width = panel.shape
    owned, lanes = scaling.shape
    per_sub = width // lanes
    coarse = coarse_diag.shape[1]
    x = lax.axis_index("gx")
    y = lax.axis_index("gy")

    cand[...] = jnp.zeros_like(cand)
    inbox[...] = jnp.zeros_like(inbox)

    barrier = pltpu.get_barrier_semaphore()
    for off in range(1, nx):
        pl.semaphore_signal(barrier, inc=1, device_id=(lax.rem(x + off, nx), y), device_id_type=MESH)
    for off in range(1, ny):
        pl.semaphore_signal(barrier, inc=1, device_id=(x, lax.rem(y + off, ny)), device_id_type=MESH)

    start = rhs[...]
    base_w = [start]
    base_y = [scaling[...] * start]
    cand[0, pl.ds(0, owned), :] = base_y[0]

    total = None
    for s in range(slots):
        live = jnp.where(counts[0, 0] > s, 1.0, 0.0)
        hot = lax.broadcasted_iota(jnp.int32, (coarse, corner.shape[1]), 0) == corner_map[s : s + 1, :]
        local = jnp.dot(
            hot.astype(jnp.float32).astype(jnp.bfloat16), corner[s], preferred_element_type=jnp.float32
        )
        local = local * live
        expand[s] = local.T
        term = lax.dot_general(
            local, local, (((1,), (1,)), ((), ())), precision=HIGHEST, preferred_element_type=jnp.float32
        )
        total = term if total is None else total + term
    part[0] = total

    pl.semaphore_wait(barrier, nx + ny - 2)

    sides = [
        (x < nx - 1, (x + 1, y)),
        (x > 0, (x - 1, y)),
        (y < ny - 1, (x, y + 1)),
        (y > 0, (x, y - 1)),
    ]
    opposite = [1, 0, 3, 2]

    def halo_copy(k, d):
        return pltpu.make_async_remote_copy(
            src_ref=cand.at[k, pl.ds(0, owned)],
            dst_ref=cand.at[k, pl.ds((1 + opposite[d]) * owned, owned)],
            send_sem=halo_send.at[k, d],
            recv_sem=halo_recv.at[k, opposite[d]],
            device_id=sides[d][1],
            device_id_type=MESH,
        )

    def back_copy(k, d):
        return pltpu.make_async_remote_copy(
            src_ref=contrib.at[k, d],
            dst_ref=inbox.at[k, opposite[d]],
            send_sem=back_send.at[k, d],
            recv_sem=back_recv.at[k, opposite[d]],
            device_id=sides[d][1],
            device_id_type=MESH,
        )

    def halo_arrival(k, d):
        return pltpu.make_async_remote_copy(
            src_ref=cand.at[k, pl.ds(0, owned)],
            dst_ref=cand.at[k, pl.ds((1 + d) * owned, owned)],
            send_sem=halo_send.at[k, d],
            recv_sem=halo_recv.at[k, d],
            device_id=sides[d][1],
            device_id_type=MESH,
        )

    def back_arrival(k, d):
        return pltpu.make_async_remote_copy(
            src_ref=contrib.at[k, d],
            dst_ref=inbox.at[k, d],
            send_sem=back_send.at[k, d],
            recv_sem=back_recv.at[k, d],
            device_id=sides[d][1],
            device_id_type=MESH,
        )

    def each_side(action):
        for d in range(4):
            @pl.when(sides[d][0])
            def _(d=d):
                action(d)

    def along_y(buf, off, send, recv):
        return pltpu.make_async_remote_copy(
            src_ref=buf.at[0],
            dst_ref=buf.at[off],
            send_sem=send.at[off],
            recv_sem=recv.at[off],
            device_id=(x, lax.rem(y + off, ny)),
            device_id_type=MESH,
        )

    def along_x(buf, off, send, recv):
        return pltpu.make_async_remote_copy(
            src_ref=buf.at[0],
            dst_ref=buf.at[off],
            send_sem=send.at[off],
            recv_sem=recv.at[off],
            device_id=(lax.rem(x + off, nx), y),
            device_id_type=MESH,
        )

    each_side(lambda d: halo_copy(0, d).start())
    mat_copies = [along_y(part, off, mat_send, mat_recv) for off in range(1, ny)]
    for copy in mat_copies:
        copy.start()

    for s in range(slots):
        wide[s] = panel[s].astype(jnp.float32)
    signs = []
    for s in range(slots):
        live = jnp.where(counts[0, 0] > s, 1.0, 0.0)
        here = map_rows[s : s + 1, :]
        sign_row = jnp.where(here < owned, live, -live)
        hit = lax.broadcasted_iota(jnp.int32, (5 * owned, per_sub), 0) == here
        table = jnp.where(hit, sign_row, 0.0)
        for b in range(per_sub):
            pick[s, b] = jnp.broadcast_to(table[:, b : b + 1], (5 * owned, lanes))
        signs.append([jnp.where(block_map[s, b] < owned, live, -live) for b in range(per_sub)])

    zero_y = jnp.where(y == 0, 1.0, 0.0)
    waits = []
    for k in range(ITERS):
        each_side(lambda d: halo_arrival(k, d).wait_recv())
        values, inner = [], []
        gsum = None
        for s in range(slots):
            held = [
                cand[k, pl.ds(block_map[s, b], 1), :] * signs[s][b] for b in range(per_sub)
            ]
            acc = None
            for b in range(per_sub):
                term = wide[s, :, b * lanes : (b + 1) * lanes] * held[b]
                acc = term if acc is None else acc + term
            col = jnp.sum(acc, axis=1, keepdims=True)
            term = jnp.sum(expand[s] * col, axis=0, keepdims=True)
            gsum = term if gsum is None else gsum + term
            values.append(held)
            inner.append(col)
        gbuf = gpart.at[k]
        gbuf[0] = gsum
        copies = [along_y(gbuf, off, g_send.at[k], g_recv.at[k]) for off in range(1, ny)]
        for copy in copies:
            copy.start()
        waits.extend(copies)
        if k == 0:
            for copy in mat_copies:
                copy.wait()
            full = part[0]
            for off in range(1, ny):
                full = full + part[off]
            eye = lax.broadcasted_iota(jnp.int32, (coarse, coarse), 0) == lax.broadcasted_iota(
                jnp.int32, (coarse, coarse), 1
            )
            mat[...] = full + jnp.where(eye, coarse_diag[...], 0.0)
            if coarse == 128:
                invert_tile(mat, 0)
            else:
                @pl.loop(0, coarse // 128)
                def _(tile):
                    invert_tile(mat, tile)
            for s in range(slots):
                spread[s] = jnp.dot(
                    expand[s], mat[...], precision=HIGHEST, preferred_element_type=jnp.float32
                )
        for copy in copies:
            copy.wait_recv()
        gall = gbuf[0]
        for off in range(1, ny):
            gall = gall + gbuf[off]
        total = None
        energy = None
        for s in range(slots):
            if k == ITERS - 1:
                more = jnp.sum(inner[s] * inner[s], axis=0, keepdims=True) * (1.0 / lanes)
                more = jnp.broadcast_to(more, (1, lanes))
                for b in range(per_sub):
                    more = more + diag[s : s + 1, b * lanes : (b + 1) * lanes] * (
                        values[s][b] * values[s][b]
                    )
                energy = more if energy is None else energy + more
            col = inner[s] + jnp.sum(spread[s] * gall, axis=1, keepdims=True)
            for b in range(per_sub):
                piece = jnp.sum(
                    wide[s, :, b * lanes : (b + 1) * lanes] * col, axis=0, keepdims=True
                )
                piece = piece + diag[s : s + 1, b * lanes : (b + 1) * lanes] * values[s][b]
                term = pick[s, b] * piece
                total = term if total is None else total + term
        for d in range(4):
            contrib[k, d] = total[(1 + d) * owned : (2 + d) * owned, :]
        each_side(lambda d: back_copy(k, d).start())
        image = base_y[k] + total[:owned, :]
        if k == ITERS - 1:
            sol = jnp.dot(
                jnp.broadcast_to(gall, (8, coarse)),
                mat[...],
                precision=HIGHEST,
                preferred_element_type=jnp.float32,
            )[0:1, :]
            work = gall * sol * zero_y
            for c in range(coarse // lanes):
                energy = energy + work[:, c * lanes : (c + 1) * lanes]
            energy = energy + jnp.sum(base_y[k] * base_y[k], axis=0, keepdims=True)
            moments = [
                jnp.sum(base_w[i // 2 + i % 2] * base_y[i // 2], axis=0, keepdims=True)
                for i in range(2 * ITERS - 1)
            ] + [energy * SCALE]
            for i in range(2 * ITERS):
                red_x[0, i : i + 1, :] = moments[i]
            x_copies = [along_x(red_x, off, rx_send, rx_recv) for off in range(1, nx)]
            for copy in x_copies:
                copy.start()
        each_side(lambda d: back_arrival(k, d).wait_recv())
        for d in range(4):
            image = image + inbox[k, d]
        base_w.append(image * SCALE)
        if k < ITERS - 1:
            base_y.append(scaling[...] * base_w[-1])
            cand[k + 1, pl.ds(0, owned), :] = base_y[-1]
            each_side(lambda d: halo_copy(k + 1, d).start())

    for copy in x_copies:
        copy.wait_recv()
    summed = red_x[0]
    for off in range(1, nx):
        summed = summed + red_x[off]
    red_y[0] = summed
    y_copies = [along_y(red_y, off, ry_send, ry_recv) for off in range(1, ny)]
    for copy in y_copies:
        copy.start()
    for copy in y_copies:
        copy.wait_recv()
    summed = red_y[0]
    for off in range(1, ny):
        summed = summed + red_y[off]
    summed = jnp.broadcast_to(jnp.sum(summed, axis=1, keepdims=True), summed.shape)
    mult, res = combine([summed[i : i + 1, :] for i in range(2 * ITERS)])
    out = base_y[0] * mult[0]
    for i in range(1, ITERS):
        out = out + base_y[i] * mult[i]
    mult_out[...] = out
    out = base_w[0] * res[0]
    for i in range(1, ITERS + 1):
        out = out + base_w[i] * res[i]
    res_out[...] = out

    for k in range(ITERS):
        each_side(lambda d: halo_copy(k, d).wait_send())
        each_side(lambda d: back_copy(k, d).wait_send())
    for copy in waits + x_copies + y_copies:
        copy.wait_send()


def shards(
    nx,
    ny,
    panel,
    corner_panel,
    interface_diag,
    coarse_diag,
    scaling,
    dual_rhs,
    block_map,
    corner_map,
    counts,
):
    slots, rows, width = panel.shape[2:]
    owned, lanes = scaling.shape[2:]
    per_sub = width // lanes
    coarse = coarse_diag.shape[1]
    vmem = pl.BlockSpec(memory_space=pltpu.VMEM)
    smem = pl.BlockSpec(memory_space=pltpu.SMEM)
    f32 = jnp.float32
    dma = pltpu.SemaphoreType.DMA
    out = jax.ShapeDtypeStruct((owned, lanes), f32)
    mult, res = pl.pallas_call(
        functools.partial(kernel, nx, ny),
        out_shape=(out, out),
        in_specs=[smem, smem] + [vmem] * 8,
        out_specs=(vmem, vmem),
        scratch_shapes=[
            pltpu.VMEM((ITERS, 5 * owned, lanes), f32),
            pltpu.VMEM((ITERS, 4, owned, lanes), f32),
            pltpu.VMEM((ITERS, 4, owned, lanes), f32),
            pltpu.VMEM((slots, rows, width), f32),
            pltpu.VMEM((slots, per_sub, 5 * owned, lanes), f32),
            pltpu.VMEM((ny, coarse, coarse), f32),
            pltpu.VMEM((coarse, coarse), f32),
            pltpu.VMEM((slots, rows, coarse), f32),
            pltpu.VMEM((slots, rows, coarse), f32),
            pltpu.VMEM((ITERS, ny, 1, coarse), f32),
            pltpu.VMEM((nx, 2 * ITERS, lanes), f32),
            pltpu.VMEM((ny, 2 * ITERS, lanes), f32),
            dma((ITERS, 4)),
            dma((ITERS, 4)),
            dma((ITERS, 4)),
            dma((ITERS, 4)),
            dma((ny,)),
            dma((ny,)),
            dma((ITERS, ny)),
            dma((ITERS, ny)),
            dma((nx,)),
            dma((nx,)),
            dma((ny,)),
            dma((ny,)),
        ],
        compiler_params=pltpu.CompilerParams(
            collective_id=0, has_side_effects=True, vmem_limit_bytes=56 * 2**20
        ),
    )(
        block_map[0, 0],
        counts,
        panel[0, 0],
        corner_panel[0, 0],
        interface_diag[0, 0],
        coarse_diag,
        scaling[0, 0],
        dual_rhs[0, 0],
        block_map[0, 0],
        corner_map[0, 0],
    )
    return mult[None, None], res[None, None]


def solution(mesh):
    nx, ny = mesh.shape["gx"], mesh.shape["gy"]
    return jax.shard_map(
        functools.partial(shards, nx, ny),
        mesh=mesh,
        in_specs=(
            P("gx", "gy", None, None, None),
            P("gx", "gy", None, None, None),
            P("gx", "gy", None, None),
            P("gx", None),
            P("gx", "gy", None, None),
            P("gx", "gy", None, None),
            P("gx", "gy", None, None),
            P("gx", "gy", None, None),
            P("gx", "gy"),
        ),
        out_specs=(P("gx", "gy", None, None), P("gx", "gy", None, None)),
        check_vma=False,
    )
```

```python
import functools

import jax
import jax.numpy as jnp
from jax import lax
from jax.experimental import pallas as pl
from jax.experimental.pallas import tpu as pltpu
from jax.sharding import PartitionSpec as P

ITERS = 3
SCALE = 2.0**-8
MESH = pl.DeviceIdType.MESH
HIGHEST = lax.Precision.HIGHEST


def invert_tile(mat, tile):
    size = mat.shape[0]
    base = tile * 128
    if not isinstance(base, int):
        base = pl.multiple_of(base, 128)
    lanes = lax.broadcasted_iota(jnp.int32, (8, size), 1) - base
    subs = lax.broadcasted_iota(jnp.int32, (8, size), 0)
    narrow = lax.broadcasted_iota(jnp.int32, (8, 128), 0)
    for block in range(16):
        first = 8 * block
        rows = mat[pl.ds(base + first, 8), :]
        small = mat[pl.ds(base + first, 8), pl.ds(base, 128)]
        cols = [
            jnp.broadcast_to(small[:, first + c : first + c + 1], (8, 128)) for c in range(8)
        ]
        inside = (lanes >= first) & (lanes < first + 8)
        rows = jnp.where(inside, (lanes - first == subs).astype(jnp.float32), rows)
        for k in range(8):
            inverse = 1.0 / cols[k][k : k + 1, :]
            factor = cols[k]
            scaled = rows[k : k + 1, :] * jnp.tile(inverse, (1, size // 128))
            wide = jnp.tile(factor, (1, size // 128))
            rows = jnp.where(subs == k, scaled, rows - wide * scaled)
            for c in range(k + 1, 8):
                own = cols[c][k : k + 1, :] * inverse
                cols[c] = jnp.where(narrow == k, own, cols[c] - factor * own)

        def update(start, count):
            panel = mat[pl.ds(start, count), pl.ds(base, 128)]
            old = mat[pl.ds(start, count), :]
            total = jnp.where(inside[0:1, :], 0.0, old)
            for c in range(8):
                total = total - panel[:, first + c : first + c + 1] * rows[c : c + 1, :]
            mat[pl.ds(start, count), :] = total

        if size == 128:
            update(0, size)
        else:
            @pl.loop(0, size // 8)
            def _(chunk):
                update(pl.multiple_of(chunk * 8, 8), 8)

        mat[pl.ds(base + first, 8), :] = rows


def combine(moments):
    inverse_scale = 1.0 / SCALE
    res = [jnp.ones_like(moments[0])]
    direc = [jnp.ones_like(moments[0])]
    mult = []
    norm = moments[0]

    def form(left, right, shift):
        total = None
        for i, a in enumerate(left):
            for j, b in enumerate(right):
                term = a * b * moments[i + j + shift]
                total = term if total is None else total + term
        return total

    for step in range(ITERS):
        energy = form(direc, direc, 1) * inverse_scale
        alpha = norm / energy
        mult = [
            (mult[i] if i < len(mult) else 0.0) + alpha * direc[i] for i in range(len(direc))
        ]
        image = [None] + [d * inverse_scale for d in direc]
        res = [
            (res[i] if i < len(res) else 0.0)
            - (alpha * image[i] if image[i] is not None else 0.0)
            for i in range(len(image))
        ]
        if step < ITERS - 1:
            after = form(res, res, 0)
            beta = after / norm
            direc = [res[i] + (beta * direc[i] if i < len(direc) else 0.0) for i in range(len(res))]
            norm = after
    return mult, res


def kernel(
    nx,
    ny,
    block_map,
    counts,
    panel_hbm,
    corner,
    diag,
    coarse_diag,
    scaling,
    rhs,
    map_rows,
    corner_map,
    mult_out,
    res_out,
    cand,
    contrib,
    inbox,
    wide,
    pick,
    part,
    mat,
    expand,
    spread,
    gpart,
    red_x,
    halo_send,
    halo_recv,
    back_send,
    back_recv,
    mat_send,
    mat_recv,
    g_send,
    g_recv,
    rx_send,
    rx_recv,
    panel,
    load_sem,
):
    slots, rows, width = panel.shape
    load = pltpu.make_async_copy(panel_hbm, panel, load_sem)
    load.start()
    owned, lanes = scaling.shape
    per_sub = width // lanes
    coarse = coarse_diag.shape[1]
    x = lax.axis_index("gx")
    y = lax.axis_index("gy")

    cand[...] = jnp.zeros_like(cand)
    inbox[...] = jnp.zeros_like(inbox)

    barrier = pltpu.get_barrier_semaphore()
    for off in range(1, nx):
        pl.semaphore_signal(barrier, inc=1, device_id=(lax.rem(x + off, nx), y), device_id_type=MESH)
    for off in range(1, ny):
        pl.semaphore_signal(barrier, inc=1, device_id=(x, lax.rem(y + off, ny)), device_id_type=MESH)

    start = rhs[...]
    base_w = [start]
    base_y = [scaling[...] * start]
    cand[0, pl.ds(0, owned), :] = base_y[0]

    ncor = corner.shape[1]
    total_cor = slots * ncor
    for s in range(slots):
        live = jnp.where(counts[0, 0] > s, 1.0, 0.0)
        hot = lax.broadcasted_iota(jnp.int32, (coarse, ncor), 0) == corner_map[s : s + 1, :]
        gram = lax.dot_general(
            corner[s], corner[s], (((1,), (1,)), ((), ())), preferred_element_type=jnp.float32
        )
        part[0, s * ncor : (s + 1) * ncor, :] = lax.dot_general(
            gram * live,
            hot.astype(jnp.float32),
            (((1,), (1,)), ((), ())),
            precision=HIGHEST,
            preferred_element_type=jnp.float32,
        )
        for r in range(8):
            part[0, total_cor + r : total_cor + r + 1, s * ncor : (s + 1) * ncor] = corner_map[
                s : s + 1, :
            ].astype(jnp.float32)

    pl.semaphore_wait(barrier, nx + ny - 2)

    sides = [
        (x < nx - 1, (x + 1, y)),
        (x > 0, (x - 1, y)),
        (y < ny - 1, (x, y + 1)),
        (y > 0, (x, y - 1)),
    ]
    opposite = [1, 0, 3, 2]

    def halo_copy(k, d):
        return pltpu.make_async_remote_copy(
            src_ref=cand.at[k, pl.ds(0, owned)],
            dst_ref=cand.at[k, pl.ds((1 + opposite[d]) * owned, owned)],
            send_sem=halo_send.at[k, d],
            recv_sem=halo_recv.at[k, opposite[d]],
            device_id=sides[d][1],
            device_id_type=MESH,
        )

    def back_copy(k, d):
        return pltpu.make_async_remote_copy(
            src_ref=contrib.at[k, d],
            dst_ref=inbox.at[k, opposite[d]],
            send_sem=back_send.at[k, d],
            recv_sem=back_recv.at[k, opposite[d]],
            device_id=sides[d][1],
            device_id_type=MESH,
        )

    def halo_arrival(k, d):
        return pltpu.make_async_remote_copy(
            src_ref=cand.at[k, pl.ds(0, owned)],
            dst_ref=cand.at[k, pl.ds((1 + d) * owned, owned)],
            send_sem=halo_send.at[k, d],
            recv_sem=halo_recv.at[k, d],
            device_id=sides[d][1],
            device_id_type=MESH,
        )

    def back_arrival(k, d):
        return pltpu.make_async_remote_copy(
            src_ref=contrib.at[k, d],
            dst_ref=inbox.at[k, d],
            send_sem=back_send.at[k, d],
            recv_sem=back_recv.at[k, d],
            device_id=sides[d][1],
            device_id_type=MESH,
        )

    def each_side(action):
        for d in range(4):
            @pl.when(sides[d][0])
            def _(d=d):
                action(d)

    def along_y(buf, off, send, recv):
        return pltpu.make_async_remote_copy(
            src_ref=buf.at[0],
            dst_ref=buf.at[off],
            send_sem=send.at[off],
            recv_sem=recv.at[off],
            device_id=(x, lax.rem(y + off, ny)),
            device_id_type=MESH,
        )

    def along_x(buf, off, send, recv):
        return pltpu.make_async_remote_copy(
            src_ref=buf.at[0],
            dst_ref=buf.at[off],
            send_sem=send.at[off],
            recv_sem=recv.at[off],
            device_id=(lax.rem(x + off, nx), y),
            device_id_type=MESH,
        )

    each_side(lambda d: halo_copy(0, d).start())
    mat_copies = [along_y(part, off, mat_send, mat_recv) for off in range(1, ny)]
    for copy in mat_copies:
        copy.start()

    for s in range(slots):
        live = jnp.where(counts[0, 0] > s, 1.0, 0.0)
        hot = lax.broadcasted_iota(jnp.int32, (coarse, ncor), 0) == corner_map[s : s + 1, :]
        local = jnp.dot(
            hot.astype(jnp.float32).astype(jnp.bfloat16), corner[s], preferred_element_type=jnp.float32
        )
        expand[s] = (local * live).T

    load.wait()
    for s in range(slots):
        wide[s] = panel[s].astype(jnp.float32)
    signs = []
    for s in range(slots):
        live = jnp.where(counts[0, 0] > s, 1.0, 0.0)
        here = map_rows[s : s + 1, :]
        sign_row = jnp.where(here < owned, live, -live)
        hit = lax.broadcasted_iota(jnp.int32, (5 * owned, per_sub), 0) == here
        table = jnp.where(hit, sign_row, 0.0)
        for b in range(per_sub):
            pick[s, b] = jnp.broadcast_to(table[:, b : b + 1], (5 * owned, lanes))
        signs.append([jnp.where(block_map[s, b] < owned, live, -live) for b in range(per_sub)])

    waits = []
    for k in range(ITERS):
        if k == ITERS - 1:
            known = [
                jnp.sum(base_w[i // 2 + i % 2] * base_y[i // 2], axis=0, keepdims=True)
                for i in range(2 * ITERS - 1)
            ]
        each_side(lambda d: halo_arrival(k, d).wait_recv())
        values, inner = [], []
        gsum = None
        for s in range(slots):
            held = [
                cand[k, pl.ds(block_map[s, b], 1), :] * signs[s][b] for b in range(per_sub)
            ]
            acc = None
            for b in range(per_sub):
                term = wide[s, :, b * lanes : (b + 1) * lanes] * held[b]
                acc = term if acc is None else acc + term
            col = jnp.sum(acc, axis=1, keepdims=True)
            term = jnp.sum(expand[s] * col, axis=0, keepdims=True)
            gsum = term if gsum is None else gsum + term
            values.append(held)
            inner.append(col)
        gbuf = gpart.at[k]
        if k < ITERS - 1:
            gbuf[0] = jnp.broadcast_to(gsum, gbuf.shape[1:])
        else:
            energy = jnp.sum(base_y[k] * base_y[k], axis=0, keepdims=True)
            for s in range(slots):
                more = jnp.sum(inner[s] * inner[s], axis=0, keepdims=True) * (1.0 / lanes)
                energy = energy + jnp.broadcast_to(more, (1, lanes))
                for b in range(per_sub):
                    energy = energy + diag[s : s + 1, b * lanes : (b + 1) * lanes] * (
                        values[s][b] * values[s][b]
                    )
            gbuf[0] = jnp.broadcast_to(gsum, gbuf.shape[1:])
            for i in range(2 * ITERS - 1):
                gbuf[0, i + 1 : i + 2, 0:lanes] = known[i]
            gbuf[0, 2 * ITERS : 2 * ITERS + 1, 0:lanes] = energy * SCALE
        copies = [along_y(gbuf, off, g_send.at[k], g_recv.at[k]) for off in range(1, ny)]
        for copy in copies:
            copy.start()
        waits.extend(copies)
        if k == 0:
            for copy in mat_copies:
                copy.wait_recv()
            waits.extend(mat_copies)
            dofs = jnp.concatenate(
                [part[off, total_cor : total_cor + 1, 0:total_cor] for off in range(ny)], axis=1
            ).astype(jnp.int32)
            all_hot = lax.broadcasted_iota(jnp.int32, (coarse, ny * total_cor), 0) == dofs
            full = jnp.dot(
                all_hot.astype(jnp.float32),
                jnp.concatenate([part[off, 0:total_cor, :] for off in range(ny)], axis=0),
                precision=HIGHEST,
                preferred_element_type=jnp.float32,
            )
            eye = lax.broadcasted_iota(jnp.int32, (coarse, coarse), 0) == lax.broadcasted_iota(
                jnp.int32, (coarse, coarse), 1
            )
            mat[...] = full + jnp.where(eye, coarse_diag[...], 0.0)
            if coarse == 128:
                invert_tile(mat, 0)
            else:
                @pl.loop(0, coarse // 128)
                def _(tile):
                    invert_tile(mat, tile)
            for s in range(slots):
                spread[s] = jnp.dot(
                    expand[s], mat[...], precision=HIGHEST, preferred_element_type=jnp.float32
                )
        for copy in copies:
            copy.wait_recv()
        gathered = gbuf[0]
        for off in range(1, ny):
            gathered = gathered + gbuf[off]
        gall = gathered[0:1, :]
        total = None
        for s in range(slots):
            col = inner[s] + jnp.sum(spread[s] * gall, axis=1, keepdims=True)
            for b in range(per_sub):
                piece = jnp.sum(
                    wide[s, :, b * lanes : (b + 1) * lanes] * col, axis=0, keepdims=True
                )
                piece = piece + diag[s : s + 1, b * lanes : (b + 1) * lanes] * values[s][b]
                term = pick[s, b] * piece
                total = term if total is None else total + term
        for d in range(4):
            contrib[k, d] = total[(1 + d) * owned : (2 + d) * owned, :]
        each_side(lambda d: back_copy(k, d).start())
        image = base_y[k] + total[:owned, :]
        if k == ITERS - 1:
            sol = jnp.dot(
                jnp.broadcast_to(gall, (8, coarse)),
                mat[...],
                precision=HIGHEST,
                preferred_element_type=jnp.float32,
            )[0:1, :]
            work = gall * sol
            energy = gathered[2 * ITERS : 2 * ITERS + 1, 0:lanes]
            for c in range(coarse // lanes):
                energy = energy + work[:, c * lanes : (c + 1) * lanes] * SCALE
            red_x[0] = gathered[1 : 2 * ITERS + 1, 0:lanes]
            red_x[0, 2 * ITERS - 1 : 2 * ITERS, :] = energy
            x_copies = [along_x(red_x, off, rx_send, rx_recv) for off in range(1, nx)]
            for copy in x_copies:
                copy.start()
        each_side(lambda d: back_arrival(k, d).wait_recv())
        for d in range(4):
            image = image + inbox[k, d]
        base_w.append(image * SCALE)
        if k < ITERS - 1:
            base_y.append(scaling[...] * base_w[-1])
            cand[k + 1, pl.ds(0, owned), :] = base_y[-1]
            each_side(lambda d: halo_copy(k + 1, d).start())

    for copy in x_copies:
        copy.wait_recv()
    summed = red_x[0]
    for off in range(1, nx):
        summed = summed + red_x[off]
    summed = jnp.broadcast_to(jnp.sum(summed, axis=1, keepdims=True), summed.shape)
    mult, res = combine([summed[i : i + 1, :] for i in range(2 * ITERS)])
    out = base_y[0] * mult[0]
    for i in range(1, ITERS):
        out = out + base_y[i] * mult[i]
    mult_out[...] = out
    out = base_w[0] * res[0]
    for i in range(1, ITERS + 1):
        out = out + base_w[i] * res[i]
    res_out[...] = out

    for k in range(ITERS):
        each_side(lambda d: halo_copy(k, d).wait_send())
        each_side(lambda d: back_copy(k, d).wait_send())
    for copy in waits + x_copies:
        copy.wait_send()


def shards(
    nx,
    ny,
    panel,
    corner_panel,
    interface_diag,
    coarse_diag,
    scaling,
    dual_rhs,
    block_map,
    corner_map,
    counts,
):
    slots, rows, width = panel.shape[2:]
    owned, lanes = scaling.shape[2:]
    per_sub = width // lanes
    coarse = coarse_diag.shape[1]
    ncor = corner_panel.shape[3]
    vmem = pl.BlockSpec(memory_space=pltpu.VMEM)
    smem = pl.BlockSpec(memory_space=pltpu.SMEM)
    f32 = jnp.float32
    dma = pltpu.SemaphoreType.DMA
    out = jax.ShapeDtypeStruct((owned, lanes), f32)
    mult, res = pl.pallas_call(
        functools.partial(kernel, nx, ny),
        out_shape=(out, out),
        in_specs=[smem, smem, pl.BlockSpec(memory_space=pltpu.HBM)] + [vmem] * 7,
        out_specs=(vmem, vmem),
        scratch_shapes=[
            pltpu.VMEM((ITERS, 5 * owned, lanes), f32),
            pltpu.VMEM((ITERS, 4, owned, lanes), f32),
            pltpu.VMEM((ITERS, 4, owned, lanes), f32),
            pltpu.VMEM((slots, rows, width), f32),
            pltpu.VMEM((slots, per_sub, 5 * owned, lanes), f32),
            pltpu.VMEM((ny, slots * ncor + 8, coarse), f32),
            pltpu.VMEM((coarse, coarse), f32),
            pltpu.VMEM((slots, rows, coarse), f32),
            pltpu.VMEM((slots, rows, coarse), f32),
            pltpu.VMEM((ITERS, ny, 2 * ITERS + 2, coarse), f32),
            pltpu.VMEM((nx, 2 * ITERS, lanes), f32),
            dma((ITERS, 4)),
            dma((ITERS, 4)),
            dma((ITERS, 4)),
            dma((ITERS, 4)),
            dma((ny,)),
            dma((ny,)),
            dma((ITERS, ny)),
            dma((ITERS, ny)),
            dma((nx,)),
            dma((nx,)),
            pltpu.VMEM((slots, rows, width), panel.dtype),
            dma,
        ],
        compiler_params=pltpu.CompilerParams(
            collective_id=0, has_side_effects=True, vmem_limit_bytes=56 * 2**20
        ),
    )(
        block_map[0, 0],
        counts,
        panel[0, 0],
        corner_panel[0, 0],
        interface_diag[0, 0],
        coarse_diag,
        scaling[0, 0],
        dual_rhs[0, 0],
        block_map[0, 0],
        corner_map[0, 0],
    )
    return mult[None, None], res[None, None]


def solution(mesh):
    nx, ny = mesh.shape["gx"], mesh.shape["gy"]
    return jax.shard_map(
        functools.partial(shards, nx, ny),
        mesh=mesh,
        in_specs=(
            P("gx", "gy", None, None, None),
            P("gx", "gy", None, None, None),
            P("gx", "gy", None, None),
            P("gx", None),
            P("gx", "gy", None, None),
            P("gx", "gy", None, None),
            P("gx", "gy", None, None),
            P("gx", "gy", None, None),
            P("gx", "gy"),
        ),
        out_specs=(P("gx", "gy", None, None), P("gx", "gy", None, None)),
        check_vma=False,
    )
```

```python
import functools

import jax
import jax.numpy as jnp
from jax import lax
from jax.experimental import pallas as pl
from jax.experimental.pallas import tpu as pltpu
from jax.sharding import PartitionSpec as P

ITERS = 3
SCALE = 2.0**-8
MESH = pl.DeviceIdType.MESH
HIGHEST = lax.Precision.HIGHEST


def invert_tile(mat, tile):
    size = mat.shape[0]
    base = tile * 128
    if not isinstance(base, int):
        base = pl.multiple_of(base, 128)
    lanes = lax.broadcasted_iota(jnp.int32, (8, size), 1) - base
    subs = lax.broadcasted_iota(jnp.int32, (8, size), 0)
    narrow = lax.broadcasted_iota(jnp.int32, (8, 128), 0)
    for block in range(16):
        first = 8 * block
        rows = mat[pl.ds(base + first, 8), :]
        small = mat[pl.ds(base + first, 8), pl.ds(base, 128)]
        cols = [
            jnp.broadcast_to(small[:, first + c : first + c + 1], (8, 128)) for c in range(8)
        ]
        inside = (lanes >= first) & (lanes < first + 8)
        rows = jnp.where(inside, (lanes - first == subs).astype(jnp.float32), rows)
        for k in range(8):
            inverse = 1.0 / cols[k][k : k + 1, :]
            factor = cols[k]
            scaled = rows[k : k + 1, :] * jnp.tile(inverse, (1, size // 128))
            wide = jnp.tile(factor, (1, size // 128))
            rows = jnp.where(subs == k, scaled, rows - wide * scaled)
            for c in range(k + 1, 8):
                own = cols[c][k : k + 1, :] * inverse
                cols[c] = jnp.where(narrow == k, own, cols[c] - factor * own)

        def update(start, count):
            panel = mat[pl.ds(start, count), pl.ds(base, 128)]
            old = mat[pl.ds(start, count), :]
            total = jnp.where(inside[0:1, :], 0.0, old)
            for c in range(8):
                total = total - panel[:, first + c : first + c + 1] * rows[c : c + 1, :]
            mat[pl.ds(start, count), :] = total

        if size == 128:
            update(0, size)
        else:
            @pl.loop(0, size // 8)
            def _(chunk):
                update(pl.multiple_of(chunk * 8, 8), 8)

        mat[pl.ds(base + first, 8), :] = rows


def combine(moments):
    inverse_scale = 1.0 / SCALE
    res = [jnp.ones_like(moments[0])]
    direc = [jnp.ones_like(moments[0])]
    mult = []
    norm = moments[0]

    def form(left, right, shift):
        total = None
        for i, a in enumerate(left):
            for j, b in enumerate(right):
                term = a * b * moments[i + j + shift]
                total = term if total is None else total + term
        return total

    for step in range(ITERS):
        energy = form(direc, direc, 1) * inverse_scale
        alpha = norm / energy
        mult = [
            (mult[i] if i < len(mult) else 0.0) + alpha * direc[i] for i in range(len(direc))
        ]
        image = [None] + [d * inverse_scale for d in direc]
        res = [
            (res[i] if i < len(res) else 0.0)
            - (alpha * image[i] if image[i] is not None else 0.0)
            for i in range(len(image))
        ]
        if step < ITERS - 1:
            after = form(res, res, 0)
            beta = after / norm
            direc = [res[i] + (beta * direc[i] if i < len(direc) else 0.0) for i in range(len(res))]
            norm = after
    return mult, res


def kernel(
    nx,
    ny,
    block_map,
    counts,
    panel_hbm,
    corner,
    diag,
    coarse_diag,
    scaling,
    rhs,
    map_rows,
    corner_map,
    mult_out,
    res_out,
    cand,
    contrib,
    inbox,
    wide,
    pick,
    part,
    mat,
    expand,
    spread,
    gfirst,
    gpart,
    red_x,
    halo_send,
    halo_recv,
    back_send,
    back_recv,
    mat_send,
    mat_recv,
    g_send,
    g_recv,
    rx_send,
    rx_recv,
    panel,
    load_sem,
):
    slots, rows, width = panel.shape
    load = pltpu.make_async_copy(panel_hbm, panel, load_sem)
    load.start()
    owned, lanes = scaling.shape
    per_sub = width // lanes
    coarse = coarse_diag.shape[1]
    x = lax.axis_index("gx")
    y = lax.axis_index("gy")

    barrier = pltpu.get_barrier_semaphore()
    for off in range(1, nx):
        pl.semaphore_signal(barrier, inc=1, device_id=(lax.rem(x + off, nx), y), device_id_type=MESH)
    for off in range(1, ny):
        pl.semaphore_signal(barrier, inc=1, device_id=(x, lax.rem(y + off, ny)), device_id_type=MESH)

    start = rhs[...]
    base_w = [start]
    base_y = [scaling[...] * start]
    cand[0, pl.ds(0, owned), :] = base_y[0]

    ncor = corner.shape[1]
    total_cor = slots * ncor
    for s in range(slots):
        live = jnp.where(counts[0, 0] > s, 1.0, 0.0)
        hot = lax.broadcasted_iota(jnp.int32, (coarse, ncor), 0) == corner_map[s : s + 1, :]
        gram = lax.dot_general(
            corner[s], corner[s], (((1,), (1,)), ((), ())), preferred_element_type=jnp.float32
        )
        part[0, s * ncor : (s + 1) * ncor, :] = lax.dot_general(
            gram * live,
            hot.astype(jnp.float32),
            (((1,), (1,)), ((), ())),
            precision=HIGHEST,
            preferred_element_type=jnp.float32,
        )
        for r in range(8):
            part[0, total_cor + r : total_cor + r + 1, s * ncor : (s + 1) * ncor] = corner_map[
                s : s + 1, :
            ].astype(jnp.float32)

    pl.semaphore_wait(barrier, nx + ny - 2)

    low, high = y == 0, y == ny - 1
    if nx % 2 == 0:
        pair = x + 1 - 2 * lax.rem(x, 2)
        up = (jnp.where(high, pair, x), jnp.where(high, y, y + 1))
        down = (jnp.where(low, pair, x), jnp.where(low, y, y - 1))
        up_slot, down_slot = jnp.where(high, 2, 3), jnp.where(low, 3, 2)
    else:
        up, down = (x, lax.rem(y + 1, ny)), (x, lax.rem(y + ny - 1, ny))
        up_slot, down_slot = 3, 2
    sides = [
        ((lax.rem(x + 1, nx), y), 1),
        ((lax.rem(x + nx - 1, nx), y), 0),
        (up, up_slot),
        (down, down_slot),
    ]
    ones = [jnp.where(there, 1.0, 0.0) for there in (x < nx - 1, x > 0, y < ny - 1, y > 0)]

    def halo_copy(k, d):
        peer, slot = sides[d]
        return pltpu.make_async_remote_copy(
            src_ref=cand.at[k, pl.ds(0, owned)],
            dst_ref=cand.at[k, pl.ds((1 + slot) * owned, owned)],
            send_sem=halo_send.at[k, d],
            recv_sem=halo_recv.at[k, slot],
            device_id=peer,
            device_id_type=MESH,
        )

    def back_copy(k, d):
        peer, slot = sides[d]
        return pltpu.make_async_remote_copy(
            src_ref=contrib.at[k, d],
            dst_ref=inbox.at[k, slot],
            send_sem=back_send.at[k, d],
            recv_sem=back_recv.at[k, slot],
            device_id=peer,
            device_id_type=MESH,
        )

    def halo_arrival(k, d):
        return pltpu.make_async_remote_copy(
            src_ref=cand.at[k, pl.ds(0, owned)],
            dst_ref=cand.at[k, pl.ds((1 + d) * owned, owned)],
            send_sem=halo_send.at[k, d],
            recv_sem=halo_recv.at[k, d],
            device_id=sides[d][0],
            device_id_type=MESH,
        )

    def back_arrival(k, d):
        return pltpu.make_async_remote_copy(
            src_ref=contrib.at[k, d],
            dst_ref=inbox.at[k, d],
            send_sem=back_send.at[k, d],
            recv_sem=back_recv.at[k, d],
            device_id=sides[d][0],
            device_id_type=MESH,
        )

    def each_side(action):
        for d in range(4):
            action(d)

    def sign_of(target, live):
        sign = jnp.where(target < owned, live, -live)
        for d in range(4):
            on_side = (target >= (1 + d) * owned) & (target < (2 + d) * owned)
            sign = jnp.where(on_side, sign * ones[d], sign)
        return sign

    def along_y(buf, off, send, recv):
        return pltpu.make_async_remote_copy(
            src_ref=buf.at[0],
            dst_ref=buf.at[off],
            send_sem=send.at[off],
            recv_sem=recv.at[off],
            device_id=(x, lax.rem(y + off, ny)),
            device_id_type=MESH,
        )

    def along_x(buf, off, send, recv):
        return pltpu.make_async_remote_copy(
            src_ref=buf.at[0],
            dst_ref=buf.at[off],
            send_sem=send.at[off],
            recv_sem=recv.at[off],
            device_id=(lax.rem(x + off, nx), y),
            device_id_type=MESH,
        )

    each_side(lambda d: halo_copy(0, d).start())
    mat_copies = [along_y(part, off, mat_send, mat_recv) for off in range(1, ny)]
    for copy in mat_copies:
        copy.start()

    for s in range(slots):
        live = jnp.where(counts[0, 0] > s, 1.0, 0.0)
        hot = lax.broadcasted_iota(jnp.int32, (coarse, ncor), 0) == corner_map[s : s + 1, :]
        local = jnp.dot(
            hot.astype(jnp.float32).astype(jnp.bfloat16), corner[s], preferred_element_type=jnp.float32
        )
        expand[s] = (local * live).T

    load.wait()
    for s in range(slots):
        wide[s] = panel[s].astype(jnp.float32)
    signs = []
    for s in range(slots):
        live = jnp.where(counts[0, 0] > s, 1.0, 0.0)
        here = map_rows[s : s + 1, :]
        sign_row = sign_of(here, live)
        hit = lax.broadcasted_iota(jnp.int32, (5 * owned, per_sub), 0) == here
        table = jnp.where(hit, sign_row, 0.0)
        for b in range(per_sub):
            pick[s, b] = jnp.broadcast_to(table[:, b : b + 1], (5 * owned, lanes))
        signs.append([sign_of(block_map[s, b], live) for b in range(per_sub)])

    waits = []
    for k in range(ITERS):
        if k == ITERS - 1:
            known = [
                jnp.sum(base_w[i // 2 + i % 2] * base_y[i // 2], axis=0, keepdims=True)
                for i in range(2 * ITERS - 1)
            ]
        each_side(lambda d: halo_arrival(k, d).wait_recv())
        values, inner = [], []
        gsum = None
        for s in range(slots):
            held = [
                cand[k, pl.ds(block_map[s, b], 1), :] * signs[s][b] for b in range(per_sub)
            ]
            acc = None
            for b in range(per_sub):
                term = wide[s, :, b * lanes : (b + 1) * lanes] * held[b]
                acc = term if acc is None else acc + term
            col = jnp.sum(acc, axis=1, keepdims=True)
            term = jnp.sum(expand[s] * col, axis=0, keepdims=True)
            gsum = term if gsum is None else gsum + term
            values.append(held)
            inner.append(col)
        gbuf = gpart if k == ITERS - 1 else gfirst.at[k]
        if k < ITERS - 1:
            gbuf[0] = gsum
        else:
            energy = jnp.sum(base_y[k] * base_y[k], axis=0, keepdims=True)
            for s in range(slots):
                more = jnp.sum(inner[s] * inner[s], axis=0, keepdims=True) * (1.0 / lanes)
                energy = energy + jnp.broadcast_to(more, (1, lanes))
                for b in range(per_sub):
                    energy = energy + diag[s : s + 1, b * lanes : (b + 1) * lanes] * (
                        values[s][b] * values[s][b]
                    )
            gbuf[0] = jnp.broadcast_to(gsum, gbuf.shape[1:])
            for i in range(2 * ITERS - 1):
                gbuf[0, i + 1 : i + 2, 0:lanes] = known[i]
            gbuf[0, 2 * ITERS : 2 * ITERS + 1, 0:lanes] = energy * SCALE
        copies = [along_y(gbuf, off, g_send.at[k], g_recv.at[k]) for off in range(1, ny)]
        for copy in copies:
            copy.start()
        waits.extend(copies)
        if k == 0:
            for copy in mat_copies:
                copy.wait_recv()
            waits.extend(mat_copies)
            dofs = jnp.concatenate(
                [part[off, total_cor : total_cor + 1, 0:total_cor] for off in range(ny)], axis=1
            ).astype(jnp.int32)
            all_hot = lax.broadcasted_iota(jnp.int32, (coarse, ny * total_cor), 0) == dofs
            full = jnp.dot(
                all_hot.astype(jnp.float32),
                jnp.concatenate([part[off, 0:total_cor, :] for off in range(ny)], axis=0),
                precision=HIGHEST,
                preferred_element_type=jnp.float32,
            )
            eye = lax.broadcasted_iota(jnp.int32, (coarse, coarse), 0) == lax.broadcasted_iota(
                jnp.int32, (coarse, coarse), 1
            )
            mat[...] = full + jnp.where(eye, coarse_diag[...], 0.0)
            if coarse == 128:
                invert_tile(mat, 0)
            else:
                @pl.loop(0, coarse // 128)
                def _(tile):
                    invert_tile(mat, tile)
            for s in range(slots):
                spread[s] = jnp.dot(
                    expand[s], mat[...], precision=HIGHEST, preferred_element_type=jnp.float32
                )
        for copy in copies:
            copy.wait_recv()
        gathered = gbuf[0]
        for off in range(1, ny):
            gathered = gathered + gbuf[off]
        gall = gathered[0:1, :]
        total = None
        for s in range(slots):
            col = inner[s] + jnp.sum(spread[s] * gall, axis=1, keepdims=True)
            for b in range(per_sub):
                piece = jnp.sum(
                    wide[s, :, b * lanes : (b + 1) * lanes] * col, axis=0, keepdims=True
                )
                piece = piece + diag[s : s + 1, b * lanes : (b + 1) * lanes] * values[s][b]
                term = pick[s, b] * piece
                total = term if total is None else total + term
        for d in range(4):
            contrib[k, d] = total[(1 + d) * owned : (2 + d) * owned, :]
        each_side(lambda d: back_copy(k, d).start())
        image = base_y[k] + total[:owned, :]
        if k == ITERS - 1:
            sol = jnp.dot(
                jnp.broadcast_to(gall, (8, coarse)),
                mat[...],
                precision=HIGHEST,
                preferred_element_type=jnp.float32,
            )[0:1, :]
            work = gall * sol
            energy = gathered[2 * ITERS : 2 * ITERS + 1, 0:lanes]
            for c in range(coarse // lanes):
                energy = energy + work[:, c * lanes : (c + 1) * lanes] * SCALE
            red_x[0] = gathered[1 : 2 * ITERS + 1, 0:lanes]
            red_x[0, 2 * ITERS - 1 : 2 * ITERS, :] = energy
            x_copies = [along_x(red_x, off, rx_send, rx_recv) for off in range(1, nx)]
            for copy in x_copies:
                copy.start()
        each_side(lambda d: back_arrival(k, d).wait_recv())
        for d in range(4):
            image = image + inbox[k, d]
        base_w.append(image * SCALE)
        if k < ITERS - 1:
            base_y.append(scaling[...] * base_w[-1])
            cand[k + 1, pl.ds(0, owned), :] = base_y[-1]
            each_side(lambda d: halo_copy(k + 1, d).start())

    for copy in x_copies:
        copy.wait_recv()
    summed = red_x[0]
    for off in range(1, nx):
        summed = summed + red_x[off]
    summed = jnp.broadcast_to(jnp.sum(summed, axis=1, keepdims=True), summed.shape)
    mult, res = combine([summed[i : i + 1, :] for i in range(2 * ITERS)])
    out = base_y[0] * mult[0]
    for i in range(1, ITERS):
        out = out + base_y[i] * mult[i]
    mult_out[...] = out
    out = base_w[0] * res[0]
    for i in range(1, ITERS + 1):
        out = out + base_w[i] * res[i]
    res_out[...] = out

    for k in range(ITERS):
        each_side(lambda d: halo_copy(k, d).wait_send())
        each_side(lambda d: back_copy(k, d).wait_send())
    for copy in waits + x_copies:
        copy.wait_send()


def shards(
    nx,
    ny,
    panel,
    corner_panel,
    interface_diag,
    coarse_diag,
    scaling,
    dual_rhs,
    block_map,
    corner_map,
    counts,
):
    slots, rows, width = panel.shape[2:]
    owned, lanes = scaling.shape[2:]
    per_sub = width // lanes
    coarse = coarse_diag.shape[1]
    ncor = corner_panel.shape[3]
    vmem = pl.BlockSpec(memory_space=pltpu.VMEM)
    smem = pl.BlockSpec(memory_space=pltpu.SMEM)
    f32 = jnp.float32
    dma = pltpu.SemaphoreType.DMA
    out = jax.ShapeDtypeStruct((owned, lanes), f32)
    mult, res = pl.pallas_call(
        functools.partial(kernel, nx, ny),
        out_shape=(out, out),
        in_specs=[smem, smem, pl.BlockSpec(memory_space=pltpu.HBM)] + [vmem] * 7,
        out_specs=(vmem, vmem),
        scratch_shapes=[
            pltpu.VMEM((ITERS, 5 * owned, lanes), f32),
            pltpu.VMEM((ITERS, 4, owned, lanes), f32),
            pltpu.VMEM((ITERS, 4, owned, lanes), f32),
            pltpu.VMEM((slots, rows, width), f32),
            pltpu.VMEM((slots, per_sub, 5 * owned, lanes), f32),
            pltpu.VMEM((ny, slots * ncor + 8, coarse), f32),
            pltpu.VMEM((coarse, coarse), f32),
            pltpu.VMEM((slots, rows, coarse), f32),
            pltpu.VMEM((slots, rows, coarse), f32),
            pltpu.VMEM((ITERS - 1, ny, 1, coarse), f32),
            pltpu.VMEM((ny, 2 * ITERS + 2, coarse), f32),
            pltpu.VMEM((nx, 2 * ITERS, lanes), f32),
            dma((ITERS, 4)),
            dma((ITERS, 4)),
            dma((ITERS, 4)),
            dma((ITERS, 4)),
            dma((ny,)),
            dma((ny,)),
            dma((ITERS, ny)),
            dma((ITERS, ny)),
            dma((nx,)),
            dma((nx,)),
            pltpu.VMEM((slots, rows, width), panel.dtype),
            dma,
        ],
        compiler_params=pltpu.CompilerParams(
            collective_id=0, has_side_effects=True, vmem_limit_bytes=56 * 2**20
        ),
    )(
        block_map[0, 0],
        counts,
        panel[0, 0],
        corner_panel[0, 0],
        interface_diag[0, 0],
        coarse_diag,
        scaling[0, 0],
        dual_rhs[0, 0],
        block_map[0, 0],
        corner_map[0, 0],
    )
    return mult[None, None], res[None, None]


def solution(mesh):
    nx, ny = mesh.shape["gx"], mesh.shape["gy"]
    return jax.shard_map(
        functools.partial(shards, nx, ny),
        mesh=mesh,
        in_specs=(
            P("gx", "gy", None, None, None),
            P("gx", "gy", None, None, None),
            P("gx", "gy", None, None),
            P("gx", None),
            P("gx", "gy", None, None),
            P("gx", "gy", None, None),
            P("gx", "gy", None, None),
            P("gx", "gy", None, None),
            P("gx", "gy"),
        ),
        out_specs=(P("gx", "gy", None, None), P("gx", "gy", None, None)),
        check_vma=False,
    )
```
